1024 devices in a mesh: grp: 8 (over y), elem: 128 (over x, z, core).
Axes of the slice: x: 4, y: 8, z: 16, core: 2. Of those that a mesh axis runs over, the one named last changes fastest.
Arguments:
- residual: float32 [64, 1024, 512], P('grp', 'elem'), may hold values from -6 to 6
- basis: float32 [3, 10, 10], replicated, may hold values from -2 to 2
- eigen: float32 [3, 10], replicated, may hold values from 0.3 to 3
- wall_scale: float32 [128], replicated, may hold values from 0.5 to 4
- coarse_weight: float32 [8, 8, 8], replicated, may hold values from -0.25 to 0.25
- row_map: int32 [8, 128, 64], P('grp', 'elem'), may hold values from 0 to 2047
- factor: float32 [8, 2048, 2048], P('grp', 'elem'), as said below
Outputs:
- correction: float32 [64, 1024, 512], P('grp', 'elem')
The draws below stay inside these ranges and needn't reach their ends.
Inputs may be any that keep to these rules, and one draw needn't show every extreme that they name: row_map names a coarse row of the element's own group. Each factor[g] is lower triangular with a positive diagonal.
All inputs are finite; a program needn't handle non-finite values.
Results may differ from the reference program's by a relative error of at most 0.0001.
Values sent between devices are 32-bit elements; how exact they have to be, the bound alone decides.
No kernel may reach another device: no remote copies, remote signals or barrier semaphores. Data moves between devices by JAX's collectives and lax.ppermute only.
A program may use at most 32 MiB of HBM per device.

```python
import math
import jax
import jax.numpy as jnp
from jax import lax

NODES = 8
BOX = 10
EX = 1
GX = 8
GY = 128
GZ = 64
NODES_X = 64
NODES_Y = 1024
NODES_Z = 512
COARSE = 2048
GROUPS = 8


def draw_factor(key, part):
    noise_key, diag_key = jax.random.split(jax.random.fold_in(key, 11))
    noise = jax.random.normal(noise_key, (GROUPS, COARSE, COARSE), jnp.float32) / math.sqrt(COARSE)
    diagonal = jnp.exp(jax.random.uniform(diag_key, (GROUPS, COARSE), jnp.float32, -0.7, 0.7))
    row_pos = lax.broadcasted_iota(jnp.int32, (COARSE, COARSE), 0)
    col_pos = lax.broadcasted_iota(jnp.int32, (COARSE, COARSE), 1)
    lower = jnp.where((row_pos > col_pos)[None], noise, 0.0)
    return lower + jnp.where((row_pos == col_pos)[None], diagonal[:, :, None], 0.0)


def touch_ends(values, key, least, largest):
    spot = [jax.random.randint(jax.random.fold_in(key, axis), (), 0, length) for axis, length in enumerate(values.shape)]
    widest = values.shape.index(max(values.shape))
    next_to = spot[:widest] + [(spot[widest] + 1) % values.shape[widest]] + spot[widest + 1:]
    return values.at[tuple(spot)].set(least).at[tuple(next_to)].set(largest)


def level_of(own_key, shape, cuts, least, high):
    factor_of, own = 1.0, jax.random.fold_in(own_key, 6)
    for position, shards_of in cuts:
        steps = jnp.exp(jax.random.uniform(jax.random.fold_in(own, position), (shards_of,), jnp.float32, least / len(cuts), high / len(cuts)))
        factor_of = factor_of * jnp.repeat(steps, shape[position] // shards_of).reshape([-1 if axis == position else 1 for axis in range(len(shape))])
    return factor_of


def normal_values(stream_key, shape, deviation, most, pieces=(), kind=jnp.bfloat16):
    gain = level_of(stream_key, shape, pieces, -0.22, 0.18) if pieces else 1.0
    drawn = jax.random.normal(stream_key, shape, jnp.float32) * deviation * gain
    return jnp.minimum(jnp.maximum(drawn, -most), most).astype(kind)


def setup_inputs(seed: int = 0) -> dict:
    streams_of = jax.random.split(jax.random.key(seed), 8)
    residual = normal_values(streams_of[0], (NODES_X, NODES_Y, NODES_Z), 1.0, 6.0, ((0, 8), (1, 128)), jnp.float32)
    basis = normal_values(streams_of[1], (3, BOX, BOX), BOX ** -0.5, 2.0, (), jnp.float32)
    eigen = jnp.clip(jnp.exp(jax.random.uniform(streams_of[2], (3, BOX), jnp.float32, math.log(0.3), math.log(3.0))), 0.3, 3.0)
    wall_scale = jnp.clip(jnp.exp(jax.random.uniform(streams_of[3], (GY,), jnp.float32, math.log(0.5), math.log(4.0))), 0.5, 4.0)
    coarse_weight = normal_values(streams_of[4], (NODES, NODES, NODES), (NODES**3) ** -0.5, 0.25, (), jnp.float32)
    row_map = touch_ends(jax.random.randint(streams_of[5], (GX, GY, GZ), 0, COARSE), jax.random.fold_in(streams_of[5], 1), 0, COARSE - 1).astype(jnp.int32)
    factor = draw_factor(jax.random.fold_in(streams_of[7], 71), 0)
    return dict(residual=residual, basis=basis, eigen=eigen, wall_scale=wall_scale, coarse_weight=coarse_weight, row_map=row_map, factor=factor)


highest = lax.Precision.HIGHEST


def face_mask(box_width):
    positions = jnp.arange(box_width)
    on_rim = ((positions == 0) | (positions == box_width - 1)).astype(jnp.int32)
    rim_count = on_rim[:, None, None] + on_rim[None, :, None] + on_rim[None, None, :]
    return (rim_count <= 1).astype(jnp.float32)[:, :, :, None, None, None]


def extract_boxes(padded):
    box_width = NODES + 2
    count_x = (padded.shape[0] - 2) // NODES
    count_y = (padded.shape[1] - 2) // NODES
    count_z = (padded.shape[2] - 2) // NODES
    along_x = jnp.stack([padded[offset:offset + NODES * count_x:NODES] for offset in range(box_width)], 0)
    along_y = jnp.stack([along_x[:, :, offset:offset + NODES * count_y:NODES] for offset in range(box_width)], 1)
    return jnp.stack([along_y[:, :, :, :, offset:offset + NODES * count_z:NODES] for offset in range(box_width)], 2)


def solve_boxes(boxed, basis, eigen, wall_rows):
    box_mask = face_mask(NODES + 2)
    spectral = boxed * box_mask
    spectral = jnp.einsum('pi,pqrxyz->iqrxyz', basis[0], spectral, precision=highest)
    spectral = jnp.einsum('qj,iqrxyz->ijrxyz', basis[1], spectral, precision=highest)
    spectral = jnp.einsum('rk,ijrxyz->ijkxyz', basis[2], spectral, precision=highest)
    divisor = (eigen[0][:, None, None, None, None, None]
               + eigen[1][None, :, None, None, None, None] * wall_rows[None, None, None, None, :, None]
               + eigen[2][None, None, :, None, None, None])
    scaled = spectral / divisor
    scaled = jnp.einsum('ip,pqrxyz->iqrxyz', basis[0], scaled, precision=highest)
    scaled = jnp.einsum('jq,iqrxyz->ijrxyz', basis[1], scaled, precision=highest)
    scaled = jnp.einsum('kr,ijrxyz->ijkxyz', basis[2], scaled, precision=highest)
    return scaled * box_mask


def place_last(core_rows, lower_rim, upper_rim):
    lead_shape = core_rows.shape[:-2]
    elements = core_rows.shape[-2]
    length = elements * NODES
    widths = [(0, 0)] * len(lead_shape)
    middle = jnp.pad(core_rows.reshape(lead_shape + (length,)), widths + [(1, 1)])
    zero_cols = jnp.zeros(lead_shape + (elements, NODES - 1), core_rows.dtype)
    lower_part = jnp.concatenate([lower_rim[..., None], zero_cols], -1).reshape(lead_shape + (length,))
    upper_part = jnp.concatenate([zero_cols, upper_rim[..., None]], -1).reshape(lead_shape + (length,))
    return middle + jnp.pad(lower_part, widths + [(0, 2)]) + jnp.pad(upper_part, widths + [(2, 0)])


def spread_boxes(solved):
    along_z = place_last(jnp.moveaxis(solved[:, :, 1:-1], 2, -1), solved[:, :, 0], solved[:, :, -1])
    along_y = place_last(jnp.transpose(along_z[:, 1:-1], (0, 2, 4, 3, 1)),
                         jnp.transpose(along_z[:, 0], (0, 1, 3, 2)),
                         jnp.transpose(along_z[:, -1], (0, 1, 3, 2)))
    along_y = jnp.swapaxes(along_y, -1, -2)
    along_x = place_last(jnp.transpose(along_y[1:-1], (2, 3, 1, 0)),
                         jnp.transpose(along_y[0], (1, 2, 0)),
                         jnp.transpose(along_y[-1], (1, 2, 0)))
    return jnp.transpose(along_x, (2, 0, 1))


def local_solve(padded, basis, eigen, wall_rows):
    return spread_boxes(solve_boxes(extract_boxes(padded), basis, eigen, wall_rows))


def reference(residual, basis, eigen, wall_scale, coarse_weight, row_map, factor):
    padded = jnp.pad(residual, 1)

    def slab_step(column, total_sum):
        start = (column * NODES).astype(jnp.int32)
        slab = lax.dynamic_slice_in_dim(padded, start, NODES + 2, 0)
        update = local_solve(slab, basis, eigen, wall_scale)
        current = lax.dynamic_slice_in_dim(total_sum, start, NODES + 2, 0)
        return lax.dynamic_update_slice_in_dim(total_sum, current + update, start, 0)

    total_sum = lax.fori_loop(0, GX, slab_step, jnp.zeros_like(padded))
    local_part = total_sum[1:-1, 1:-1, 1:-1]
    blocks = residual.reshape(GX, NODES, GY, NODES, GZ, NODES)
    element_res = jnp.einsum('xaybzc,abc->xyz', blocks, coarse_weight, precision=highest)
    grouped = element_res.reshape(GROUPS, EX * GY * GZ)
    row_ids = row_map.reshape(GROUPS, EX * GY * GZ).astype(jnp.int32)

    def coarse_group(inputs):
        element_vals, group_ids, group_factor = inputs
        right_side = jax.ops.segment_sum(element_vals, group_ids, num_segments=COARSE)
        halfway = jnp.dot(group_factor, right_side, precision=highest)
        return jnp.dot(halfway, group_factor, precision=highest)

    solution = lax.map(coarse_group, (grouped, row_ids, factor))
    values = jnp.take_along_axis(solution, row_ids, axis=1).reshape(GX, GY, GZ)
    coarse_field = (values[:, None, :, None, :, None] * coarse_weight[None, :, None, :, None, :]).reshape(NODES_X, NODES_Y, NODES_Z)
    return local_part + coarse_field
```

```python
import jax
import jax.numpy as jnp
from jax import lax
from jax.experimental import pallas as pl
from jax.experimental.pallas import tpu as pltpu
from jax.sharding import PartitionSpec as P

N = 8
BOX = N + 2
CH = 128
SLOT = 16
PER = CH // N
WIDE = PER * SLOT

f32 = jnp.float32
bf16 = jnp.bfloat16
i32 = jnp.int32
HI = lax.Precision.HIGHEST
NN = (((1,), (0,)), ((), ()))
NT = (((1,), (1,)), ((), ()))


def iota(shape, axis):
    return lax.broadcasted_iota(i32, shape, axis)


def exact(a, b, dims=NN):
    return lax.dot_general(a, b, dims, precision=HI, preferred_element_type=f32)


def fast(a, b, dims=NN):
    return lax.dot_general(a, b, dims, preferred_element_type=f32)


def pick(cond):
    return cond.astype(f32)


def split3(v):
    one = v.astype(bf16).astype(f32)
    rest = v - one
    two = rest.astype(bf16).astype(f32)
    return one, two, rest - two


def tiled_weight(cw, nz):
    return exact(cw, pick(iota((N, nz), 0) == (iota((N, nz), 1) & (N - 1))))


def residual_kernel(r_ref, cw_ref, map_ref, send_ref, xl_ref, xh_ref, yl_ref, yh_ref):
    rows, nz = r_ref.shape
    peers, width = send_ref.shape
    elements = nz // N
    r = r_ref[...]
    xl_ref[...] = r[:N]
    xh_ref[...] = r[rows - N :]
    yl_ref[...] = jnp.concatenate([r[N * x : N * x + 1] for x in range(N)], 0)
    yh_ref[...] = jnp.concatenate([r[N * x + N - 1 : N * x + N] for x in range(N)], 0)
    part = r * tiled_weight(cw_ref[...], nz)
    total = jnp.sum(part, axis=0, keepdims=True)
    grouping = pick((iota((nz, width), 0) >> 3) == iota((nz, width), 1))
    values = exact(jnp.broadcast_to(total, (8, nz)), grouping)
    shift = pick(iota((elements, width), 0) + elements == iota((elements, width), 1))
    ids = jnp.broadcast_to(map_ref[...].astype(f32), (8, elements))
    row = values + exact(ids, shift)
    send_ref[...] = jnp.broadcast_to(row[:1], (peers, width))


def coarse_kernel(g_ref, l_ref, out_ref, a_ref, b_ref, s_ref):
    peers, width = g_ref.shape
    half = peers // 2
    quarter = width // 2
    blocks = l_ref.shape[1] // CH
    g = g_ref[...]
    top, bottom = g[:half], g[half:]
    left = iota((half, width), 1) < quarter
    values = jnp.where(left, top, pltpu.roll(bottom, quarter, 1))
    ids = jnp.where(left, pltpu.roll(top, quarter, 1), bottom).astype(i32)
    high, low = ids >> 7, ids & (CH - 1)
    pieces = split3(values)
    sub_low = iota((CH, width), 0)
    sub_high = iota((blocks, width), 0)
    for t in range(half):
        cols = slice(width * t, width * (t + 1))
        b_ref[:, cols] = pick(low[t : t + 1] == sub_low).astype(bf16)
        hit = high[t : t + 1] == sub_high
        a_ref[:, cols] = jnp.concatenate(
            [jnp.where(hit, piece[t : t + 1], 0.0) for piece in pieces], 0
        ).astype(bf16)
    summed = fast(a_ref[...], b_ref[...], NT)
    right = summed[:blocks] + summed[blocks : 2 * blocks] + summed[2 * blocks :]
    acc = jnp.zeros((l_ref.shape[0], CH), f32)
    for q in range(blocks):
        acc = acc + l_ref[:, CH * q : CH * (q + 1)] * right[q : q + 1]
    halfway = jnp.sum(acc, axis=1, keepdims=True)
    share = jnp.concatenate(
        [
            jnp.sum(l_ref[:, CH * q : CH * (q + 1)] * halfway, axis=0, keepdims=True)
            for q in range(blocks)
        ],
        0,
    )
    stacked = jnp.concatenate(split3(share), 0).astype(bf16)
    step = 8
    for t0 in range(0, half, step):
        found = fast(stacked, b_ref[:, width * t0 : width * (t0 + step)])
        found = found[:blocks] + found[blocks : 2 * blocks] + found[2 * blocks :]
        for t in range(t0, t0 + step):
            cols = slice(width * (t - t0), width * (t - t0 + 1))
            hit = high[t : t + 1] == sub_high
            s_ref[t : t + 1, :] = jnp.sum(
                jnp.where(hit, found[:, cols], 0.0), axis=0, keepdims=True
            )
    s = s_ref[...]
    out_ref[:half, :] = s
    out_ref[half:, :] = pltpu.roll(s, quarter, 1)


def local_kernel(
    wall_ref, r_ref, xm_ref, xp_ref, ym_ref, yp_ref, basis_ref, eigen_ref,
    core_ref, oxm_ref, oxp_ref, oym_ref, oyp_ref,
):
    rows, nz = r_ref.shape
    chunks = nz // CH
    wall = wall_ref[lax.axis_index("elem")]
    basis0, basis1, basis2 = basis_ref[0], basis_ref[1], basis_ref[2]
    eigen = eigen_ref[...]
    faces = 4 * N
    nodes = rows + faces
    modes = CH

    def node_at(shape, axis):
        n = iota(shape, axis)
        m = n & (N - 1)
        nx = jnp.where(n < rows, n >> 3, m) + 1
        nx = jnp.where((n >= rows) & (n < rows + N), 0, nx)
        nx = jnp.where((n >= rows + N) & (n < rows + 2 * N), BOX - 1, nx)
        ny = m + 1
        ny = jnp.where((n >= rows + 2 * N) & (n < rows + 3 * N), 0, ny)
        ny = jnp.where(n >= rows + 3 * N, BOX - 1, ny)
        return nx, ny

    def mode_at(shape, axis):
        s = iota(shape, axis)
        sx = (s * 205) >> 11
        return sx, s - BOX * sx

    rx, ry = mode_at((modes, BOX), 0)
    kx, ky = pick(rx == iota((modes, BOX), 1)), pick(ry == iota((modes, BOX), 1))
    cx, cy = node_at((BOX, nodes), 1)
    nxs, nys = pick(cx == iota((BOX, nodes), 0)), pick(cy == iota((BOX, nodes), 0))
    forward = exact(exact(kx, basis0, NT), nxs) * exact(exact(ky, basis1, NT), nys)
    bx, by = mode_at((BOX, modes), 1)
    mx, my = pick(bx == iota((BOX, modes), 0)), pick(by == iota((BOX, modes), 0))
    dx, dy = node_at((nodes, BOX), 0)
    px, py = pick(dx == iota((nodes, BOX), 1)), pick(dy == iota((nodes, BOX), 1))
    back = exact(px, exact(basis0, mx)) * exact(py, exact(basis1, my))

    lane_mode = pick((iota((BOX, WIDE), 1) & (SLOT - 1)) == iota((BOX, WIDE), 0))
    basis_lane = exact(basis2, lane_mode)
    take = pick((iota((CH, BOX), 0) & (N - 1)) + 1 == iota((CH, BOX), 1))
    own = exact(take, basis_lane)
    row = iota((CH, WIDE), 0)
    element = iota((CH, WIDE), 1) >> 4
    first, last = basis_lane[:1], basis_lane[BOX - 1 :]
    face_z = jnp.where((row >> 3) == element, own, 0.0)
    mid_z = face_z + jnp.where((row & (N - 1) == N - 1) & ((row >> 3) + 1 == element), first, 0.0)
    mid_z = mid_z + jnp.where((row & (N - 1) == 0) & ((row >> 3) - 1 == element), last, 0.0)
    prev_z = jnp.where((row == CH - 1) & (element == 0), first, 0.0)
    next_z = jnp.where((row == 0) & (element == PER - 1), last, 0.0)

    r = r_ref[...]
    blank = jnp.zeros((rows, CH), f32)
    edged = jnp.concatenate([blank, r, blank], 1)
    inner = jnp.concatenate([edged[:, CH * c : CH * (c + 3)] for c in range(chunks)], 0)
    inner = exact(inner, jnp.concatenate([prev_z, mid_z, next_z], 0))
    rim = jnp.concatenate([xm_ref[...], xp_ref[...], ym_ref[...], yp_ref[...]], 0)
    rim = jnp.concatenate([rim[:, CH * c : CH * (c + 1)] for c in range(chunks)], 0)
    rim = exact(rim, face_z)

    def beside(v, count):
        return jnp.concatenate([v[count * c : count * (c + 1)] for c in range(chunks)], 1)

    boxed = jnp.concatenate([beside(inner, rows), beside(rim, faces)], 0)
    spectral = exact(forward, boxed)
    e0 = jnp.sum(kx * eigen[0:1], axis=1, keepdims=True)
    e1 = jnp.sum(ky * eigen[1:2], axis=1, keepdims=True)
    column = jnp.where(iota((modes, 1), 0) < BOX * BOX, e0 + wall * e1, 1.0)
    line = exact(jnp.broadcast_to(eigen[2:3], (8, BOX)), lane_mode)[:1]
    scaled = spectral / (column + jnp.concatenate([line] * chunks, 1))
    solved = exact(back, scaled)

    blank = jnp.zeros((rows, WIDE), f32)
    edged = jnp.concatenate([blank, solved[:rows], blank], 1)
    inner = jnp.concatenate([edged[:, WIDE * c : WIDE * (c + 3)] for c in range(chunks)], 0)
    inner = exact(inner, jnp.concatenate([next_z, mid_z, prev_z], 1), NT)
    rim = jnp.concatenate([solved[rows:, WIDE * c : WIDE * (c + 1)] for c in range(chunks)], 0)
    rim = exact(rim, face_z, NT)
    core_ref[...] = beside(inner, rows)
    rim = beside(rim, faces)
    for i, ref in enumerate((oxm_ref, oxp_ref, oym_ref, oyp_ref)):
        ref[...] = rim[N * i : N * (i + 1)]


def final_kernel(core_ref, xl_ref, xh_ref, yl_ref, yh_ref, got_ref, cw_ref, out_ref):
    rows, nz = core_ref.shape
    width = got_ref.shape[1]
    elements = nz // N
    sol = jnp.sum(got_ref[...], axis=0, keepdims=True)
    sol = jnp.where(iota((1, width), 1) < elements, sol, 0.0)
    expand = pick(iota((width, nz), 0) == (iota((width, nz), 1) >> 3))
    sol = exact(jnp.broadcast_to(sol, (8, width)), expand)
    coarse = tiled_weight(cw_ref[...], nz)
    y = iota((N, nz), 0)
    for x in range(N):
        at = slice(N * x, N * (x + 1))
        v = core_ref[at, :] + coarse[at] * sol
        v = v + jnp.where(y == 0, yl_ref[x : x + 1, :], 0.0)
        v = v + jnp.where(y == N - 1, yh_ref[x : x + 1, :], 0.0)
        if x == 0:
            v = v + xl_ref[...]
        if x == N - 1:
            v = v + xh_ref[...]
        out_ref[at, :] = v


def vmem(count):
    return [pl.BlockSpec(memory_space=pltpu.VMEM)] * count


def shape(*dims):
    return jax.ShapeDtypeStruct(dims, f32)


def cost(flops, size):
    return pl.CostEstimate(flops=flops, bytes_accessed=size, transcendentals=0)


def per_device(residual, basis, eigen, wall_scale, coarse_weight, row_map, factor):
    nx, ny, nz = residual.shape
    rows = nx * ny
    elements = nz // N
    peers = lax.axis_size("elem")
    slabs = lax.axis_size("grp")
    width = 2 * elements
    coarse = factor.shape[2]
    r = residual.reshape(rows, nz)
    cw = coarse_weight.reshape(rows, N)
    face = shape(N, nz)

    send, xl, xh, yl, yh = pl.pallas_call(
        residual_kernel,
        out_shape=[shape(peers, width), face, face, face, face],
        in_specs=vmem(3),
        out_specs=vmem(5),
        cost_estimate=cost(1 << 22, 1 << 18),
        name="residual_kernel",
    )(r, cw, row_map.reshape(1, elements))

    def up(v, axis, count):
        return lax.ppermute(v, axis, [(i, i + 1) for i in range(count - 1)])

    def down(v, axis, count):
        return lax.ppermute(v, axis, [(i + 1, i) for i in range(count - 1)])

    xm, xp = up(xh, "grp", slabs), down(xl, "grp", slabs)
    ym, yp = up(yh, "elem", peers), down(yl, "elem", peers)

    gathered = lax.all_to_all(send, "elem", 0, 0, tiled=True)

    core, oxm, oxp, oym, oyp = pl.pallas_call(
        local_kernel,
        out_shape=[shape(rows, nz), face, face, face, face],
        in_specs=[pl.BlockSpec(memory_space=pltpu.SMEM)] + vmem(7),
        out_specs=vmem(5),
        cost_estimate=cost(1 << 30, 1 << 22),
        name="local_kernel",
    )(wall_scale, r, xm, xp, ym, yp, basis, eigen)

    gxl, gxh = up(oxp, "grp", slabs), down(oxm, "grp", slabs)
    gyl, gyh = up(oyp, "elem", peers), down(oym, "elem", peers)

    shares = pl.pallas_call(
        coarse_kernel,
        out_shape=shape(peers, width),
        in_specs=vmem(2),
        out_specs=pl.BlockSpec(memory_space=pltpu.VMEM),
        scratch_shapes=[
            pltpu.VMEM((3 * coarse // CH, peers * elements), bf16),
            pltpu.VMEM((CH, peers * elements), bf16),
            pltpu.VMEM((peers // 2, width), f32),
        ],
        cost_estimate=cost(1 << 28, 1 << 21),
        name="coarse_kernel",
    )(gathered, factor[0])
    got = lax.all_to_all(shares, "elem", 0, 0, tiled=True)

    out = pl.pallas_call(
        final_kernel,
        out_shape=shape(rows, nz),
        in_specs=vmem(7),
        out_specs=pl.BlockSpec(memory_space=pltpu.VMEM),
        cost_estimate=cost(1 << 22, 1 << 19),
        name="final_kernel",
    )(core, gxl, gxh, gyl, gyh, got, cw)
    return out.reshape(nx, ny, nz)


def solution(mesh):
    placed = (
        P("grp", "elem", None),
        P(),
        P(),
        P(),
        P(),
        P("grp", "elem", None),
        P("grp", "elem", None),
    )
    return jax.shard_map(
        per_device, mesh=mesh, in_specs=placed, out_specs=P("grp", "elem", None), check_vma=False
    )
```
